32 devices in a mesh: seq: 8 (over z, core), chan: 4 (over y, x).
Axes of the slice: x: 2, y: 2, z: 4, core: 2. Of those that a mesh axis runs over, the one named last changes fastest.
Arguments:
- gate_raw: bfloat16 [8, 2048, 2048], P('seq', None, 'chan'), may hold values from -50 to 50
- value_raw: bfloat16 [8, 2048, 2048], P('seq', None, 'chan'), may hold values from -50 to 50
- filter_gate: float32 [7, 2048], P(None, 'chan'), may hold values from -3 to 3
- filter_value: float32 [7, 2048], P(None, 'chan'), may hold values from -3 to 3
- teacher: float32 [8, 2048, 2048], P('seq', 'chan'), may hold values from -0.25 to 1, as said below
Outputs:
- grad_gate_raw: bfloat16 [8, 2048, 2048], P('seq', None, 'chan')
- grad_value_raw: bfloat16 [8, 2048, 2048], P('seq', None, 'chan')
- grad_filter_gate: float32 [7, 2048], P(None, 'chan')
- grad_filter_value: float32 [7, 2048], P(None, 'chan')
The draws below stay inside these ranges and needn't reach their ends.
Inputs may be any that keep to these rules, and one draw needn't show every extreme that they name: teacher[s] is symmetric for each of the 8 sequences, with ones on its diagonal.
All inputs are finite; a program needn't handle non-finite values.
Results may differ from the reference program's by a relative error of at most 0.0059.
Values may be sent and summed in bfloat16 or wider, within the bound.
A program may use at most 128 MiB of HBM per device.

```python
import math
import jax
import jax.numpy as jnp
from jax import lax

D = 2048
TAPS = 7
LEN = 2048
SEQS = 8


def scaled_field(key):
    key_base, key_rows, key_chan = jax.random.split(key, 3)
    extent = (SEQS, LEN, D)
    values = jnp.clip(jax.random.normal(key_base, extent, jnp.float32), -4.0, 4.0)
    ramp_span = 0.25 * math.log(3.0)
    half_decade = 0.5 * math.log(10.0)
    row_scale = jnp.exp(jax.random.uniform(key_rows, (SEQS, LEN, 1), jnp.float32, 0.0, half_decade))
    channel_ramp = jnp.arange(D, dtype=jnp.float32) * (ramp_span / D)
    chan_scale = jnp.exp(channel_ramp + jax.random.uniform(key_chan, (D,), jnp.float32, -0.22, 0.22))
    return (values * row_scale * chan_scale).astype(jnp.bfloat16)


def draw_gate_raw(key, part):
    return scaled_field(jax.random.fold_in(key, 17))


def draw_value_raw(key, part):
    return scaled_field(jax.random.fold_in(key, 23))


def draw_teacher(key, part):
    extent = (SEQS, LEN, LEN)
    noise_key = jax.random.fold_in(key, 41)
    raw_values = jnp.clip(jax.random.normal(noise_key, extent, jnp.float32), -4.0, 4.0) * 0.05
    symmetric = 0.5 * (raw_values + jnp.swapaxes(raw_values, 1, 2))
    position = jnp.arange(LEN)
    diagonal = position[:, None] == position[None, :]
    return jnp.where(diagonal, 1.0, symmetric).astype(jnp.float32)


def block_levels(own_key, dims, cuts, smallest, largest):
    level, own = 1.0, jax.random.fold_in(own_key, 6)
    for axis_at, parts in cuts:
        draws = jnp.exp(jax.random.uniform(jax.random.fold_in(own, axis_at), (parts,), jnp.float32, smallest / len(cuts), largest / len(cuts)))
        level = level * jnp.repeat(draws, dims[axis_at] // parts).reshape([-1 if axis == axis_at else 1 for axis in range(len(dims))])
    return level


def gaussian(own_key, shape, width, most, pieces=(), kind=jnp.bfloat16):
    drawn = width * jax.random.normal(own_key, shape, jnp.float32)
    if pieces:
        drawn = drawn * block_levels(own_key, shape, pieces, -0.22, 0.18)
    return jnp.clip(drawn, -most, most).astype(kind)


def setup_inputs(seed: int = 0) -> dict:
    key_list = jax.random.split(jax.random.key(seed), 6)
    return {
        "gate_raw": draw_gate_raw(jax.random.fold_in(key_list[5], 71), 0),
        "value_raw": draw_value_raw(jax.random.fold_in(key_list[5], 71), 0),
        "filter_gate": gaussian(key_list[2], (TAPS, D), 0.5, 3.0, ((1, 4),), jnp.float32),
        "filter_value": gaussian(key_list[3], (TAPS, D), 0.5, 3.0, ((1, 4),), jnp.float32),
        "teacher": draw_teacher(jax.random.fold_in(key_list[5], 71), 0),
    }


epsilon = 1e-06

def causal_conv(signal, weights):
    length = signal.shape[0]
    padded = jnp.pad(signal.astype(jnp.float32), ((TAPS - 1, 0), (0, 0)))
    summed = jnp.zeros(signal.shape, jnp.float32)
    for tap_index in range(TAPS):
        summed = summed + weights[tap_index] * padded[TAPS - 1 - tap_index:TAPS - 1 - tap_index + length]
    return summed

def adjoint_conv(upstream, weights):
    length = upstream.shape[0]
    padded = jnp.pad(upstream, ((0, TAPS - 1), (0, 0)))
    summed = jnp.zeros(upstream.shape, jnp.float32)
    for tap_index in range(TAPS):
        summed = summed + weights[tap_index] * padded[tap_index:tap_index + length]
    return summed

def tap_sums(upstream, signal):
    length = signal.shape[0]
    padded = jnp.pad(signal.astype(jnp.float32), ((TAPS - 1, 0), (0, 0)))
    return jnp.stack([lax.optimization_barrier(jnp.sum(upstream * padded[TAPS - 1 - tap_index:TAPS - 1 - tap_index + length], axis=0)) for tap_index in range(TAPS)])

def reference(gate_raw, value_raw, filter_gate, filter_value, teacher):
    factor = 16.0 / math.sqrt(LEN)

    def one_sequence(inputs):
        gate_seq, value_seq, teacher_seq = inputs
        gate_conv = causal_conv(gate_seq, filter_gate)
        value_conv = causal_conv(value_seq, filter_value)
        hidden = (gate_conv * value_conv).astype(jnp.bfloat16)
        hidden_f = hidden.astype(jnp.float32)
        inv_rms = lax.rsqrt(lax.optimization_barrier(jnp.sum(hidden_f * hidden_f, axis=1, keepdims=True)) / D + epsilon)
        normed_f = hidden_f * inv_rms
        normed = normed_f.astype(jnp.bfloat16)
        similarity = jnp.dot(normed, normed.T, preferred_element_type=jnp.float32) / D
        residue = (factor * (similarity - teacher_seq)).astype(jnp.bfloat16)
        normed_grad = jnp.dot(residue, normed, preferred_element_type=jnp.float32)
        projection = lax.optimization_barrier(jnp.sum(normed_f * normed_grad, axis=1, keepdims=True)) / D
        hidden_grad = inv_rms * (normed_grad - normed_f * projection)
        gate_conv_grad = hidden_grad * value_conv
        value_conv_grad = hidden_grad * gate_conv
        grad_gate = adjoint_conv(gate_conv_grad, filter_gate).astype(jnp.bfloat16)
        grad_value = adjoint_conv(value_conv_grad, filter_value).astype(jnp.bfloat16)
        return (grad_gate, grad_value, tap_sums(gate_conv_grad, gate_seq), tap_sums(value_conv_grad, value_seq))
    grad_gate, grad_value, gate_taps, value_taps = lax.map(one_sequence, (gate_raw, value_raw, teacher))
    norm_factor = 1.0 / math.sqrt(SEQS * LEN)
    return (grad_gate, grad_value, lax.optimization_barrier(jnp.sum(gate_taps, axis=0)) * norm_factor, lax.optimization_barrier(jnp.sum(value_taps, axis=0)) * norm_factor)
```

```python
import functools
import math

import jax
import jax.numpy as jnp
from jax import lax
from jax.experimental import pallas as pl
from jax.experimental.pallas import tpu as pltpu
from jax.sharding import PartitionSpec as P

epsilon = 1e-06
PAD = 16
TILE = 64
MESH = pl.DeviceIdType.MESH


def kernel(
    groups, rings, taps, norm_factor,
    gate_in, value_in, filter_gate, filter_value, teacher_in,
    gate_out, value_out, gate_taps, value_taps,
    raw_g, raw_v, conv_g, conv_v, held, teach, own_n, block_n, total, outgoing, hgrad,
    out_g, out_v, sums, mine, others,
    in_sem, out_sem, send_sem, recv_sem, fwd_sem, a2a_send, a2a_recv, tap_send, tap_recv,
):
    length, width = gate_in.shape[1:]
    stripe = length // groups
    full = width * groups
    factor = 16.0 / math.sqrt(length)
    tile = min(TILE, stripe)
    lanes = [slice(k, min(k + 128, width)) for k in range(0, width, 128)]
    f32, bf16 = jnp.float32, jnp.bfloat16
    me, ring = lax.axis_index("chan"), lax.axis_index("seq")
    square = groups == 4

    def rows_of(chunk, size=stripe, start=0):
        return pl.ds(pl.multiple_of(chunk * stripe + start, math.gcd(stripe, start) if start else stripe), size)

    in_copies = []
    for c in range(groups):
        span = pl.ds(c * stripe, stripe)
        dest = pl.ds(PAD + c * stripe, stripe)
        for k, (src, dst) in enumerate(((gate_in, raw_g), (value_in, raw_v))):
            in_copies.append(pltpu.make_async_copy(src.at[0, span], dst.at[dest], in_sem.at[k, c]))
    for copy in in_copies:
        copy.start()
    teach_copy = pltpu.make_async_copy(teacher_in.at[0], teach, in_sem.at[2, 0])
    teach_copy.start()

    barrier = pltpu.get_barrier_semaphore()
    for step in range(1, groups):
        pl.semaphore_signal(barrier, inc=1, device_id=(ring, lax.rem(me + step, groups)), device_id_type=MESH)
    for step in range(1, rings):
        pl.semaphore_signal(barrier, inc=1, device_id=(lax.rem(ring + step, rings), me), device_id_type=MESH)

    raw_g[0:PAD] = jnp.zeros((PAD, width), bf16)
    raw_v[0:PAD] = jnp.zeros((PAD, width), bf16)
    conv_g[length:] = jnp.zeros((PAD, width), f32)
    conv_v[length:] = jnp.zeros((PAD, width), f32)
    hgrad[length:] = jnp.zeros((PAD, width), bf16)
    sums[...] = jnp.zeros(sums.shape, f32)
    total[...] = jnp.zeros(total.shape, f32)
    for copy in in_copies:
        copy.wait()

    def conv_chunk(chunk):
        def body(i, _):
            base = pl.multiple_of(chunk * stripe + i * tile, tile)
            for lane in lanes:
                made = []
                for raw, weights, store in ((raw_g, filter_gate, conv_g), (raw_v, filter_value, conv_v)):
                    window = raw[pl.ds(base, tile + PAD), lane].astype(f32)
                    out = weights[0:1, lane] * window[PAD:]
                    for j in range(1, taps):
                        out = out + weights[j : j + 1, lane] * pltpu.roll(window, j, 0)[PAD:]
                    store[pl.ds(base, tile), lane] = out
                    made.append(out)
                held[me, pl.ds(base, tile), lane] = (made[0] * made[1]).astype(bf16)
            return 0

        lax.fori_loop(0, stripe // tile, body, 0)

    def gather_copy(source, rows, device, send, recv):
        block = held.at[source, rows]
        return pltpu.make_async_remote_copy(
            src_ref=block, dst_ref=block, send_sem=send, recv_sem=recv,
            device_id=(ring, device), device_id_type=MESH,
        )

    started = []
    if square:
        across = me + 1 - 2 * lax.rem(me, 2)
        along = lax.rem(me + 2, 4)
        corner = 3 - me

        def send(to, k, chunk):
            copy = gather_copy(me, rows_of(chunk), to, send_sem.at[k, chunk], recv_sem.at[me, chunk])
            copy.start()
            started.append(copy)

        conv_chunk(across)
        pl.semaphore_wait(barrier, groups + rings - 2)
        send(across, 0, across)
        conv_chunk(along)
        send(along, 1, along)
        conv_chunk(corner)
        send(across, 0, corner)
        send(along, 1, corner)
        send(across, 0, along)
        send(along, 1, across)
        conv_chunk(me)
        send(across, 0, me)
        send(along, 1, me)
        half = stripe // 2
        for from_x, from_y in ((me, me), (along, across), (corner, corner), (across, along)):
            for k, (source, chunk, to, start, slot) in enumerate(
                ((across, from_x, along, 0, 0), (along, from_y, across, half, 1))
            ):
                gather_copy(source, rows_of(chunk), me, send_sem.at[0, 0], recv_sem.at[source, chunk]).wait_recv()
                signal = recv_sem.at[source if slot == 0 else to, chunk]
                copy = gather_copy(source, rows_of(chunk, half, start), to, fwd_sem.at[k, chunk], signal)
                copy.start()
                started.append(copy)
    else:
        for c in range(groups):
            conv_chunk(c)
        pl.semaphore_wait(barrier, groups + rings - 2)

        def send_all(copy_do):
            def body(i, _):
                chunk, step = i // (groups - 1), 1 + lax.rem(i, groups - 1)
                copy_do(
                    gather_copy(
                        me, rows_of(chunk), lax.rem(me + step, groups),
                        send_sem.at[step, chunk], recv_sem.at[me, chunk],
                    )
                )
                return 0

            lax.fori_loop(0, groups * (groups - 1), body, 0)

        send_all(lambda copy: copy.start())

    def wait_chunk(chunk):
        if square:
            gather_copy(corner, rows_of(chunk, half), me, send_sem.at[0, 0], recv_sem.at[corner, chunk]).wait_recv()
            gather_copy(corner, rows_of(chunk, half, half), me, send_sem.at[0, 0], recv_sem.at[me, chunk]).wait_recv()
        else:
            def body(step, _):
                source = lax.rem(me + step, groups)
                gather_copy(source, rows_of(chunk), me, send_sem.at[0, 0], recv_sem.at[source, chunk]).wait_recv()
                return 0

            lax.fori_loop(1, groups, body, 0)

    norm_tile = min(32, stripe)

    def scale_of(base):
        squares = jnp.zeros((norm_tile, width), f32)
        for g in range(groups):
            block = held[g, pl.ds(base, norm_tile)].astype(f32)
            squares = squares + block * block
        return lax.rsqrt(jnp.sum(squares, axis=1, keepdims=True) / full + epsilon)

    def normalize(chunk, dest):
        def body(i, _):
            base = pl.multiple_of(chunk * stripe + i * norm_tile, norm_tile)
            inverse = scale_of(base)
            for g in range(groups):
                block = held[g, pl.ds(base, norm_tile)].astype(f32)
                dest[pl.ds(pl.multiple_of(i * norm_tile, norm_tile), norm_tile), g * width : (g + 1) * width] = (
                    block * inverse
                ).astype(bf16)
            return 0

        lax.fori_loop(0, stripe // norm_tile, body, 0)

    teach_copy.wait()
    mat = min(256, stripe)

    def gram_chunk(t, _):
        chunk = lax.rem(me + t, groups)
        wait_chunk(chunk)
        normalize(chunk, block_n)

        @pl.when(t == 0)
        def _():
            own_n[...] = block_n[...]

        def body(m, _):
            rows = pl.ds(pl.multiple_of(m * mat, mat), mat)
            similarity = lax.dot_general(
                own_n[rows], block_n[...], (((1,), (1,)), ((), ())), preferred_element_type=f32
            ) / full
            residue = (factor * (similarity - teach[rows, rows_of(chunk)])).astype(bf16)
            total[rows] += jnp.dot(residue, block_n[...], preferred_element_type=f32)
            return 0

        lax.fori_loop(0, stripe // mat, body, 0)
        return 0

    lax.fori_loop(0, groups, gram_chunk, 0)

    def finish(i, _):
        local = pl.multiple_of(i * norm_tile, norm_tile)
        base = pl.multiple_of(me * stripe + i * norm_tile, norm_tile)
        rows = pl.ds(local, norm_tile)
        inverse = scale_of(base)
        inner = jnp.zeros((norm_tile, width), f32)
        for g in range(groups):
            part = slice(g * width, (g + 1) * width)
            inner = inner + held[g, pl.ds(base, norm_tile)].astype(f32) * inverse * total[rows, part]
        projection = jnp.sum(inner, axis=1, keepdims=True) / full
        for g in range(groups):
            part = slice(g * width, (g + 1) * width)
            normed = held[g, pl.ds(base, norm_tile)].astype(f32) * inverse
            outgoing[g, rows] = (inverse * (total[rows, part] - normed * projection)).astype(bf16)
        return 0

    pieces = 2
    piece = stripe // pieces
    steps = piece // norm_tile

    def exchange(target, p, source_row):
        return pltpu.make_async_remote_copy(
            src_ref=outgoing.at[target, pl.ds(p * piece, piece)],
            dst_ref=hgrad.at[rows_of(source_row, piece, p * piece)],
            send_sem=a2a_send.at[target, p], recv_sem=a2a_recv.at[source_row, p],
            device_id=(ring, target), device_id_type=MESH,
        )

    for p in range(pieces):
        lax.fori_loop(p * steps, (p + 1) * steps, finish, 0)
        for step in range(1, groups):
            exchange(lax.rem(me + groups - step, groups), p, me).start()
    hgrad[rows_of(me)] = outgoing[me]

    def back_tile(base):
        for k in range(0, width, 128):
            lane = slice(k, min(k + 128, width))
            up = hgrad[pl.ds(base, tile + PAD), lane].astype(f32)
            for b, (conv, raw, weights, store) in enumerate(
                ((conv_v, raw_g, filter_gate, out_g), (conv_g, raw_v, filter_value, out_v))
            ):
                window = up * conv[pl.ds(base, tile + PAD), lane]
                signal = raw[pl.ds(pl.multiple_of(base + PAD, PAD), tile), lane].astype(f32)
                out = None
                for j in range(taps):
                    shifted = (window if j == 0 else pltpu.roll(window, tile + PAD - j, 0))[:tile]
                    term = weights[j : j + 1, lane] * shifted
                    out = term if out is None else out + term
                    product = shifted * signal
                    folded = product[0:8]
                    for r in range(8, tile, 8):
                        folded = folded + product[r : r + 8]
                    sums[b, j, :, lane] += folded
                store[pl.ds(base, tile), lane] = out.astype(bf16)

    tiles = stripe // tile
    for step in range(groups):
        source = lax.rem(me + step, groups)
        if step:
            for p in range(pieces):
                exchange_in = pltpu.make_async_remote_copy(
                    src_ref=outgoing.at[source, pl.ds(p * piece, piece)],
                    dst_ref=hgrad.at[rows_of(source, piece, p * piece)],
                    send_sem=a2a_send.at[source, p], recv_sem=a2a_recv.at[source, p],
                    device_id=(ring, source), device_id_type=MESH,
                )
                exchange_in.wait_recv()

        def inner_tiles(i, _, source=source):
            back_tile(pl.multiple_of(source * stripe + i * tile, tile))
            return 0

        lax.fori_loop(0, tiles - 1, inner_tiles, 0)

    def last_tiles(c, _):
        back_tile(pl.multiple_of(c * stripe + (tiles - 1) * tile, tile))
        return 0

    lax.fori_loop(0, groups, last_tiles, 0)
    out_copies = [
        pltpu.make_async_copy(src, dst.at[0], out_sem.at[k])
        for k, (src, dst) in enumerate(((out_g, gate_out), (out_v, value_out)))
    ]
    for copy in out_copies:
        copy.start()

    for b in range(2):
        for j in range(taps):
            mine[b, j : j + 1] = jnp.sum(sums[b, j], axis=0, keepdims=True)
        mine[b, taps:] = jnp.zeros((8 - taps, width), f32)

    def tap_copy(to, slot):
        return pltpu.make_async_remote_copy(
            src_ref=mine, dst_ref=others.at[slot], send_sem=tap_send.at[slot], recv_sem=tap_recv.at[slot],
            device_id=(to, me), device_id_type=MESH,
        )

    tap_copies = [tap_copy(lax.rem(ring + step, rings), step) for step in range(1, rings)]
    for copy in tap_copies:
        copy.start()
    summed = [mine[b] for b in range(2)]
    for step, copy in enumerate(tap_copies):
        copy.wait_recv()
        summed = [summed[b] + others[step + 1, b] for b in range(2)]
    gate_taps[...] = summed[0][:taps] * norm_factor
    value_taps[...] = summed[1][:taps] * norm_factor

    for copy in tap_copies:
        copy.wait_send()
    if square:
        for copy in started:
            copy.wait_send()
    else:
        send_all(lambda copy: copy.wait_send())
    for step in range(1, groups):
        for p in range(pieces):
            exchange(lax.rem(me + groups - step, groups), p, me).wait_send()
    for copy in out_copies:
        copy.wait()


def on_device(gate_raw, value_raw, filter_gate, filter_value, teacher):
    seq_count, length, width = gate_raw.shape
    groups, rings = lax.axis_size("chan"), lax.axis_size("seq")
    taps = filter_gate.shape[0]
    stripe, full = length // groups, width * groups
    norm_factor = 1.0 / math.sqrt(rings * seq_count * length)
    f32, bf16 = jnp.float32, jnp.bfloat16
    any_space = pl.BlockSpec(memory_space=pl.ANY)
    vmem = pl.BlockSpec(memory_space=pltpu.VMEM)
    dma = pltpu.SemaphoreType.DMA
    return pl.pallas_call(
        functools.partial(kernel, groups, rings, taps, norm_factor),
        out_shape=(
            jax.ShapeDtypeStruct(gate_raw.shape, bf16),
            jax.ShapeDtypeStruct(gate_raw.shape, bf16),
            jax.ShapeDtypeStruct((taps, width), f32),
            jax.ShapeDtypeStruct((taps, width), f32),
        ),
        in_specs=[any_space, any_space, vmem, vmem, any_space],
        out_specs=(any_space, any_space, vmem, vmem),
        scratch_shapes=[
            pltpu.VMEM((length + PAD, width), bf16),
            pltpu.VMEM((length + PAD, width), bf16),
            pltpu.VMEM((length + PAD, width), f32),
            pltpu.VMEM((length + PAD, width), f32),
            pltpu.VMEM((groups, length, width), bf16),
            pltpu.VMEM((stripe, length), f32),
            pltpu.VMEM((stripe, full), bf16),
            pltpu.VMEM((stripe, full), bf16),
            pltpu.VMEM((stripe, full), f32),
            pltpu.VMEM((groups, stripe, width), bf16),
            pltpu.VMEM((length + PAD, width), bf16),
            pltpu.VMEM((length, width), bf16),
            pltpu.VMEM((length, width), bf16),
            pltpu.VMEM((2, taps, 8, width), f32),
            pltpu.VMEM((2, 8, width), f32),
            pltpu.VMEM((rings, 2, 8, width), f32),
            dma((3, groups)),
            dma((2,)),
            dma((groups, groups)),
            dma((groups, groups)),
            dma((2, groups)),
            dma((groups, 2)),
            dma((groups, 2)),
            dma((rings,)),
            dma((rings,)),
        ],
        compiler_params=pltpu.CompilerParams(
            collective_id=0, has_side_effects=True, vmem_limit_bytes=60 * 1024 * 1024
        ),
    )(gate_raw, value_raw, filter_gate, filter_value, teacher)


def solution(mesh):
    placed = (
        P("seq", None, "chan"),
        P("seq", None, "chan"),
        P(None, "chan"),
        P(None, "chan"),
        P("seq", "chan", None),
    )
    return jax.shard_map(
        on_device,
        mesh=mesh,
        in_specs=placed,
        out_specs=(
            P("seq", None, "chan"),
            P("seq", None, "chan"),
            P(None, "chan"),
            P(None, "chan"),
        ),
        check_vma=False,
    )
```

```python
import functools
import math

import jax
import jax.numpy as jnp
from jax import lax
from jax.experimental import pallas as pl
from jax.experimental.pallas import tpu as pltpu
from jax.sharding import PartitionSpec as P

epsilon = 1e-06
PAD = 16
TILE = 64
MESH = pl.DeviceIdType.MESH


def kernel(
    groups, rings, taps, norm_factor,
    gate_in, value_in, filter_gate, filter_value, teacher_in,
    gate_out, value_out, gate_taps, value_taps,
    raw_g, raw_v, conv_g, conv_v, held, teach, own_n, block_n, total, outgoing, hgrad,
    out_g, out_v, sums, mine, others,
    in_sem, out_sem, send_sem, recv_sem, a2a_send, a2a_recv, tap_send, tap_recv,
    near, teach_send_sem, teach_recv_sem,
):
    length, width = gate_in.shape[1:]
    stripe = length // groups
    full = width * groups
    factor = 16.0 / math.sqrt(length)
    tile = min(TILE, stripe)
    lanes = [slice(k, min(k + 128, width)) for k in range(0, width, 128)]
    f32, bf16 = jnp.float32, jnp.bfloat16
    me, ring = lax.axis_index("chan"), lax.axis_index("seq")
    paired = groups == 4 and rings % 2 == 0
    flip1 = lambda at: at + 1 - 2 * lax.rem(at, 2)
    flip2 = lambda at: lax.rem(at + 2, 4)
    flip3 = lambda at: 3 - at
    if paired:
        core = lax.rem(ring, 2)
        buddy = ring + 1 - 2 * core
        side = me // 2
        same = 1 - (core - side) * (core - side)
        base_at = same * me + (1 - same) * flip2(me)
        slot = same * me + (1 - same) * groups
        proc = ring - core + side
        is_home, is_guest = same == 1, same == 0
    else:
        base_at, slot, proc = me, me, ring

    def rows_of(chunk, size=stripe, start=0):
        return pl.ds(pl.multiple_of(chunk * stripe + start, math.gcd(stripe, start) if start else stripe), size)

    in_copies = []
    for c in range(groups):
        span = pl.ds(c * stripe, stripe)
        dest = pl.ds(PAD + c * stripe, stripe)
        for k, (src, dst) in enumerate(((gate_in, raw_g), (value_in, raw_v))):
            in_copies.append(pltpu.make_async_copy(src.at[0, span], dst.at[dest], in_sem.at[k, c]))
    for copy in in_copies:
        copy.start()
    teach_copy = pltpu.make_async_copy(teacher_in.at[0], teach, in_sem.at[2, 0])
    if paired:
        pl.when(is_home)(teach_copy.start)
    else:
        teach_copy.start()

    barrier = pltpu.get_barrier_semaphore()
    for step in range(1, groups):
        pl.semaphore_signal(barrier, inc=1, device_id=(ring, lax.rem(me + step, groups)), device_id_type=MESH)
        if paired:
            pl.semaphore_signal(barrier, inc=1, device_id=(buddy, lax.rem(me + step, groups)), device_id_type=MESH)
    greeted = (groups - 1) * (2 if paired else 1) + rings - 1
    for step in range(1, rings):
        pl.semaphore_signal(barrier, inc=1, device_id=(lax.rem(ring + step, rings), me), device_id_type=MESH)

    raw_g[0:PAD] = jnp.zeros((PAD, width), bf16)
    raw_v[0:PAD] = jnp.zeros((PAD, width), bf16)
    conv_g[length:] = jnp.zeros((PAD, width), f32)
    conv_v[length:] = jnp.zeros((PAD, width), f32)
    hgrad[length:] = jnp.zeros((PAD, width), bf16)
    sums[...] = jnp.zeros(sums.shape, f32)
    total[...] = jnp.zeros(total.shape, f32)
    for copy in in_copies:
        copy.wait()

    def conv_chunk(chunk):
        def body(i, _):
            base = pl.multiple_of(chunk * stripe + i * tile, tile)
            for lane in lanes:
                made = []
                for raw, weights, store in ((raw_g, filter_gate, conv_g), (raw_v, filter_value, conv_v)):
                    window = raw[pl.ds(base, tile + PAD), lane].astype(f32)
                    out = weights[0:1, lane] * window[PAD:]
                    for j in range(1, taps):
                        out = out + weights[j : j + 1, lane] * pltpu.roll(window, j, 0)[PAD:]
                    store[pl.ds(base, tile), lane] = out
                    made.append(out)
                held[slot, pl.ds(base, tile), lane] = (made[0] * made[1]).astype(bf16)
            return 0

        lax.fori_loop(0, stripe // tile, body, 0)

    def gather_copy(source, target, chunk, to, send):
        rows = rows_of(chunk)
        return pltpu.make_async_remote_copy(
            src_ref=held.at[source, rows], dst_ref=held.at[target, rows],
            send_sem=send, recv_sem=recv_sem.at[target, chunk],
            device_id=to, device_id_type=MESH,
        )

    def arrived(source, chunk):
        gather_copy(source, source, chunk, (ring, me), send_sem.at[0, 0]).wait_recv()

    if paired:
        far = pl.ds(pl.multiple_of(side * 2 * stripe, stripe), 2 * stripe)

        def teach_send(cols, dst, to, k):
            return pltpu.make_async_remote_copy(
                src_ref=teacher_in.at[0, :, cols], dst_ref=dst, send_sem=teach_send_sem.at[k],
                recv_sem=teach_recv_sem.at[k], device_id=to, device_id_type=MESH,
            )

        to_swap = teach_send(far, teach.at[:, far], (buddy, flip2(me)), 0)
        to_near = teach_send(rows_of(flip2(me)), near.at[0], (buddy, me), 1)
        to_next = teach_send(rows_of(flip3(me)), near.at[1], (buddy, flip1(me)), 2)
        far_in = pl.ds(pl.multiple_of((1 - side) * 2 * stripe, stripe), 2 * stripe)

        def to_x(chunk):
            return gather_copy(base_at, base_at, chunk, (ring, flip1(me)), send_sem.at[0, chunk])

        def to_buddy(chunk):
            return gather_copy(base_at, base_at, chunk, (buddy, me), send_sem.at[1, chunk])

        def pass_on(chunk):
            return gather_copy(flip1(base_at), flip1(base_at), chunk, (buddy, me), send_sem.at[2, chunk])

        def swap(chunk):
            return gather_copy(groups, me, chunk, (buddy, flip2(me)), send_sem.at[3, chunk])

        order = (flip1(me), flip3(me), me, flip2(me))
        pl.semaphore_wait(barrier, greeted)

        @pl.when(is_home)
        def _():
            to_near.start()
            to_next.start()

        for chunk in order:
            conv_chunk(chunk)

            @pl.when(is_home)
            def _(chunk=chunk):
                to_x(chunk).start()
                to_buddy(chunk).start()

            @pl.when(is_guest)
            def _(chunk=chunk):
                swap(chunk).start()

        @pl.when(is_guest)
        def _():
            to_swap.start()
            for chunk in (flip3(me), flip1(me), flip2(me), me):
                arrived(base_at, chunk)
                to_x(chunk).start()
                to_buddy(chunk).start()
            for k in range(2):
                teach_send(rows_of(0), near.at[k], (ring, me), 1 + k).wait_recv()
                at = me if k == 0 else flip1(me)

                def turn(i, _, k=k, at=at):
                    rows = pl.ds(pl.multiple_of(i * 128, 128), 128)
                    for c in range(0, stripe, 128):
                        cols = pl.ds(pl.multiple_of(at * stripe + c, 128), 128)
                        teach[rows, cols] = near[k, c : c + 128, rows].T
                    return 0

                lax.fori_loop(0, stripe // 128, turn, 0)

        for chunk in (base_at, flip2(base_at)):
            arrived(flip1(base_at), chunk)
            pass_on(chunk).start()
    else:
        for c in range(groups):
            conv_chunk(c)
        pl.semaphore_wait(barrier, greeted)

        def send_all(copy_do):
            def body(i, _):
                chunk, step = i // (groups - 1), 1 + lax.rem(i, groups - 1)
                copy_do(gather_copy(me, me, chunk, (ring, lax.rem(me + step, groups)), send_sem.at[step, chunk]))
                return 0

            lax.fori_loop(0, groups * (groups - 1), body, 0)

        send_all(lambda copy: copy.start())

    def wait_chunk(t, chunk):
        if paired:
            @pl.when(t >= 2)
            def _():
                arrived(flip1(base_at), chunk)
                pass_on(chunk).start()

            arrived(flip2(base_at), chunk)
            arrived(flip3(base_at), chunk)
        else:
            def body(step, _):
                arrived(lax.rem(me + step, groups), chunk)
                return 0

            lax.fori_loop(1, groups, body, 0)

    norm_tile = min(32, stripe)

    def scale_of(base):
        squares = jnp.zeros((norm_tile, width), f32)
        for g in range(groups):
            block = held[g, pl.ds(base, norm_tile)].astype(f32)
            squares = squares + block * block
        return lax.rsqrt(jnp.sum(squares, axis=1, keepdims=True) / full + epsilon)

    def normalize(chunk, dest):
        def body(i, _):
            base = pl.multiple_of(chunk * stripe + i * norm_tile, norm_tile)
            inverse = scale_of(base)
            for g in range(groups):
                block = held[g, pl.ds(base, norm_tile)].astype(f32)
                dest[pl.ds(pl.multiple_of(i * norm_tile, norm_tile), norm_tile), g * width : (g + 1) * width] = (
                    block * inverse
                ).astype(bf16)
            return 0

        lax.fori_loop(0, stripe // norm_tile, body, 0)

    if paired:
        pl.when(is_home)(teach_copy.wait)

        @pl.when(is_guest)
        def _():
            teach_send(far_in, teach.at[:, far_in], (ring, me), 0).wait_recv()
    else:
        teach_copy.wait()
    mat = min(256, stripe)

    def gram_chunk(t, _):
        if paired:
            late = jnp.where(t == 2, flip3(me), flip1(me))
            chunk = jnp.where(t == 0, base_at, jnp.where(t == 1, flip2(base_at), late))
        else:
            chunk = lax.rem(me + t, groups)
        wait_chunk(t, chunk)
        normalize(chunk, block_n)

        @pl.when(t == 0)
        def _():
            own_n[...] = block_n[...]

        def body(m, _):
            rows = pl.ds(pl.multiple_of(m * mat, mat), mat)
            similarity = lax.dot_general(
                own_n[rows], block_n[...], (((1,), (1,)), ((), ())), preferred_element_type=f32
            ) / full
            residue = (factor * (similarity - teach[rows, rows_of(chunk)])).astype(bf16)
            total[rows] += jnp.dot(residue, block_n[...], preferred_element_type=f32)
            return 0

        lax.fori_loop(0, stripe // mat, body, 0)
        return 0

    lax.fori_loop(0, groups, gram_chunk, 0)

    def finish(i, _):
        local = pl.multiple_of(i * norm_tile, norm_tile)
        base = pl.multiple_of(base_at * stripe + i * norm_tile, norm_tile)
        rows = pl.ds(local, norm_tile)
        inverse = scale_of(base)
        inner = jnp.zeros((norm_tile, width), f32)
        for g in range(groups):
            part = slice(g * width, (g + 1) * width)
            inner = inner + held[g, pl.ds(base, norm_tile)].astype(f32) * inverse * total[rows, part]
        projection = jnp.sum(inner, axis=1, keepdims=True) / full
        for g in range(groups):
            part = slice(g * width, (g + 1) * width)
            normed = held[g, pl.ds(base, norm_tile)].astype(f32) * inverse
            outgoing[g, rows] = (inverse * (total[rows, part] - normed * projection)).astype(bf16)
        return 0

    pieces = max(1, min(4, stripe // 128))
    piece = stripe // pieces
    steps = piece // norm_tile

    def exchange(target, p, source_row):
        return pltpu.make_async_remote_copy(
            src_ref=outgoing.at[target, pl.ds(p * piece, piece)],
            dst_ref=hgrad.at[rows_of(source_row, piece, p * piece)],
            send_sem=a2a_send.at[target, p], recv_sem=a2a_recv.at[source_row, p],
            device_id=(proc, target), device_id_type=MESH,
        )

    if paired:
        targets = (flip3(me), flip1(me), flip2(me))
    else:
        targets = tuple(lax.rem(me + groups - step, groups) for step in range(1, groups))

    def stay(p):
        hgrad[rows_of(base_at, piece, p * piece)] = outgoing[me, pl.ds(p * piece, piece)]

    for p in reversed(range(pieces)):
        lax.fori_loop(p * steps, (p + 1) * steps, finish, 0)
        for target in targets:
            exchange(target, p, base_at).start()
        if paired:
            @pl.when(is_guest)
            def _(p=p):
                exchange(me, p, base_at).start()

            @pl.when(is_home)
            def _(p=p):
                stay(p)
        else:
            stay(p)

    def back_tile(base):
        for k in range(0, width, 128):
            lane = slice(k, min(k + 128, width))
            up = hgrad[pl.ds(base, tile + PAD), lane].astype(f32)
            for b, (conv, raw, weights, store) in enumerate(
                ((conv_v, raw_g, filter_gate, out_g), (conv_g, raw_v, filter_value, out_v))
            ):
                window = up * conv[pl.ds(base, tile + PAD), lane]
                signal = raw[pl.ds(pl.multiple_of(base + PAD, PAD), tile), lane].astype(f32)
                out = None
                for j in range(taps):
                    shifted = (window if j == 0 else pltpu.roll(window, tile + PAD - j, 0))[:tile]
                    term = weights[j : j + 1, lane] * shifted
                    out = term if out is None else out + term
                    product = shifted * signal
                    folded = product[0:8]
                    for r in range(8, tile, 8):
                        folded = folded + product[r : r + 8]
                    sums[b, j, :, lane] += folded
                store[pl.ds(base, tile), lane] = out.astype(bf16)

    tiles = stripe // tile
    per = tiles // pieces
    if paired:
        sources = (base_at, flip2(base_at), flip1(base_at), flip3(base_at))
    else:
        sources = tuple(lax.rem(me + step, groups) for step in range(groups))
    for p in reversed(range(pieces)):
        for step, source in enumerate(sources):
            def landed(p=p, source=source):
                exchange(source, p, source).wait_recv()

            if step:
                landed()
            elif paired:
                pl.when(is_guest)(landed)

            def inner_tiles(i, _, source=source):
                back_tile(pl.multiple_of(source * stripe + i * tile, tile))
                return 0

            lax.fori_loop(p * per, (p + 1) * per - (1 if p == pieces - 1 else 0), inner_tiles, 0)

    def last_tiles(c, _):
        back_tile(pl.multiple_of(c * stripe + (tiles - 1) * tile, tile))
        return 0

    lax.fori_loop(0, groups, last_tiles, 0)
    out_copies = [
        pltpu.make_async_copy(src, dst.at[0], out_sem.at[k])
        for k, (src, dst) in enumerate(((out_g, gate_out), (out_v, value_out)))
    ]
    for copy in out_copies:
        copy.start()

    for b in range(2):
        for j in range(taps):
            mine[b, j : j + 1] = jnp.sum(sums[b, j], axis=0, keepdims=True)
        mine[b, taps:] = jnp.zeros((8 - taps, width), f32)

    def tap_copy(to, slot):
        return pltpu.make_async_remote_copy(
            src_ref=mine, dst_ref=others.at[slot], send_sem=tap_send.at[slot], recv_sem=tap_recv.at[slot],
            device_id=(to, me), device_id_type=MESH,
        )

    tap_copies = [tap_copy(lax.rem(ring + step, rings), step) for step in range(1, rings)]
    for copy in tap_copies:
        copy.start()
    summed = [mine[b] for b in range(2)]
    for step, copy in enumerate(tap_copies):
        copy.wait_recv()
        summed = [summed[b] + others[step + 1, b] for b in range(2)]
    gate_taps[...] = summed[0][:taps] * norm_factor
    value_taps[...] = summed[1][:taps] * norm_factor

    for copy in tap_copies:
        copy.wait_send()
    if paired:
        for chunk in range(groups):
            to_x(chunk).wait_send()
            to_buddy(chunk).wait_send()
            pass_on(chunk).wait_send()

        @pl.when(is_home)
        def _():
            to_near.wait_send()
            to_next.wait_send()

        @pl.when(is_guest)
        def _():
            to_swap.wait_send()
            for chunk in range(groups):
                swap(chunk).wait_send()
            for p in range(pieces):
                exchange(me, p, base_at).wait_send()
    else:
        send_all(lambda copy: copy.wait_send())
    for target in targets:
        for p in range(pieces):
            exchange(target, p, base_at).wait_send()
    for copy in out_copies:
        copy.wait()


def on_device(gate_raw, value_raw, filter_gate, filter_value, teacher):
    seq_count, length, width = gate_raw.shape
    groups, rings = lax.axis_size("chan"), lax.axis_size("seq")
    taps = filter_gate.shape[0]
    stripe, full = length // groups, width * groups
    norm_factor = 1.0 / math.sqrt(rings * seq_count * length)
    f32, bf16 = jnp.float32, jnp.bfloat16
    any_space = pl.BlockSpec(memory_space=pl.ANY)
    vmem = pl.BlockSpec(memory_space=pltpu.VMEM)
    dma = pltpu.SemaphoreType.DMA
    return pl.pallas_call(
        functools.partial(kernel, groups, rings, taps, norm_factor),
        out_shape=(
            jax.ShapeDtypeStruct(gate_raw.shape, bf16),
            jax.ShapeDtypeStruct(gate_raw.shape, bf16),
            jax.ShapeDtypeStruct((taps, width), f32),
            jax.ShapeDtypeStruct((taps, width), f32),
        ),
        in_specs=[any_space, any_space, vmem, vmem, any_space],
        out_specs=(any_space, any_space, vmem, vmem),
        scratch_shapes=[
            pltpu.VMEM((length + PAD, width), bf16),
            pltpu.VMEM((length + PAD, width), bf16),
            pltpu.VMEM((length + PAD, width), f32),
            pltpu.VMEM((length + PAD, width), f32),
            pltpu.VMEM((groups + 1, length, width), bf16),
            pltpu.VMEM((stripe, length), f32),
            pltpu.VMEM((stripe, full), bf16),
            pltpu.VMEM((stripe, full), bf16),
            pltpu.VMEM((stripe, full), f32),
            pltpu.VMEM((groups, stripe, width), bf16),
            pltpu.VMEM((length + PAD, width), bf16),
            pltpu.VMEM((length, width), bf16),
            pltpu.VMEM((length, width), bf16),
            pltpu.VMEM((2, taps, 8, width), f32),
            pltpu.VMEM((2, 8, width), f32),
            pltpu.VMEM((rings, 2, 8, width), f32),
            dma((3, groups)),
            dma((2,)),
            dma((groups, groups)),
            dma((groups, groups)),
            dma((groups, 4)),
            dma((groups, 4)),
            dma((rings,)),
            dma((rings,)),
            pltpu.VMEM((2, stripe, stripe), f32),
            dma((3,)),
            dma((3,)),
        ],
        compiler_params=pltpu.CompilerParams(
            collective_id=0, has_side_effects=True, vmem_limit_bytes=60 * 1024 * 1024
        ),
    )(gate_raw, value_raw, filter_gate, filter_value, teacher)


def solution(mesh):
    placed = (
        P("seq", None, "chan"),
        P("seq", None, "chan"),
        P(None, "chan"),
        P(None, "chan"),
        P("seq", "chan", None),
    )
    return jax.shard_map(
        on_device,
        mesh=mesh,
        in_specs=placed,
        out_specs=(
            P("seq", None, "chan"),
            P("seq", None, "chan"),
            P(None, "chan"),
            P(None, "chan"),
        ),
        check_vma=False,
    )
```

```python
import functools
import math

import jax
import jax.numpy as jnp
from jax import lax
from jax.experimental import pallas as pl
from jax.experimental.pallas import tpu as pltpu
from jax.sharding import PartitionSpec as P

epsilon = 1e-06
PAD = 16
TILE = 64
MESH = pl.DeviceIdType.MESH


def kernel(
    groups, rings, taps, norm_factor,
    gate_in, value_in, filter_gate, filter_value, teacher_in,
    gate_out, value_out, gate_taps, value_taps,
    raw_g, raw_v, conv_g, conv_v, held, teach, own_n, block_n, total, outgoing, hgrad,
    sums, mine, others,
    in_sem, send_sem, recv_sem, a2a_send, a2a_recv, tap_send, tap_recv,
    near, teach_send_sem, teach_recv_sem,
):
    length, width = gate_in.shape[1:]
    stripe = length // groups
    full = width * groups
    factor = 16.0 / math.sqrt(length)
    tile = min(TILE, stripe)
    lanes = [slice(k, min(k + 128, width)) for k in range(0, width, 128)]
    f32, bf16 = jnp.float32, jnp.bfloat16
    me, ring = lax.axis_index("chan"), lax.axis_index("seq")
    paired = groups == 4 and rings % 2 == 0
    flip1 = lambda at: at + 1 - 2 * lax.rem(at, 2)
    flip2 = lambda at: lax.rem(at + 2, 4)
    flip3 = lambda at: 3 - at
    if paired:
        core = lax.rem(ring, 2)
        buddy = ring + 1 - 2 * core
        side = me // 2
        same = 1 - (core - side) * (core - side)
        base_at = same * me + (1 - same) * flip2(me)
        slot = same * me + (1 - same) * groups
        proc = ring - core + side
        is_home, is_guest = same == 1, same == 0
    else:
        base_at, slot, proc = me, me, ring

    def rows_of(chunk, size=stripe, start=0):
        return pl.ds(pl.multiple_of(chunk * stripe + start, math.gcd(stripe, start) if start else stripe), size)

    in_copies = []
    for c in range(groups):
        span = pl.ds(c * stripe, stripe)
        dest = pl.ds(PAD + c * stripe, stripe)
        for k, (src, dst) in enumerate(((gate_in, raw_g), (value_in, raw_v))):
            in_copies.append(pltpu.make_async_copy(src.at[0, span], dst.at[dest], in_sem.at[k, c]))
    for copy in in_copies:
        copy.start()
    teach_copy = pltpu.make_async_copy(teacher_in.at[0], teach, in_sem.at[2, 0])
    if paired:
        pl.when(is_home)(teach_copy.start)
    else:
        teach_copy.start()

    barrier = pltpu.get_barrier_semaphore()
    for step in range(1, groups):
        pl.semaphore_signal(barrier, inc=1, device_id=(ring, lax.rem(me + step, groups)), device_id_type=MESH)
        if paired:
            pl.semaphore_signal(barrier, inc=1, device_id=(buddy, lax.rem(me + step, groups)), device_id_type=MESH)
    greeted = (groups - 1) * (2 if paired else 1) + rings - 1
    for step in range(1, rings):
        pl.semaphore_signal(barrier, inc=1, device_id=(lax.rem(ring + step, rings), me), device_id_type=MESH)

    raw_g[0:PAD] = jnp.zeros((PAD, width), bf16)
    raw_v[0:PAD] = jnp.zeros((PAD, width), bf16)
    conv_g[length:] = jnp.zeros((PAD, width), f32)
    conv_v[length:] = jnp.zeros((PAD, width), f32)
    hgrad[length:] = jnp.zeros((PAD, width), bf16)
    sums[...] = jnp.zeros(sums.shape, f32)
    total[...] = jnp.zeros(total.shape, f32)
    for copy in in_copies:
        copy.wait()

    def conv_chunk(chunk):
        def body(i, _):
            base = pl.multiple_of(chunk * stripe + i * tile, tile)
            for lane in lanes:
                made = []
                for raw, weights, store in ((raw_g, filter_gate, conv_g), (raw_v, filter_value, conv_v)):
                    window = raw[pl.ds(base, tile + PAD), lane].astype(f32)
                    out = weights[0:1, lane] * window[PAD:]
                    for j in range(1, taps):
                        out = out + weights[j : j + 1, lane] * pltpu.roll(window, j, 0)[PAD:]
                    store[pl.ds(base, tile), lane] = out
                    made.append(out)
                held[slot, pl.ds(base, tile), lane] = (made[0] * made[1]).astype(bf16)
            return 0

        lax.fori_loop(0, stripe // tile, body, 0)

    def gather_copy(source, target, chunk, to, send):
        rows = rows_of(chunk)
        return pltpu.make_async_remote_copy(
            src_ref=held.at[source, rows], dst_ref=held.at[target, rows],
            send_sem=send, recv_sem=recv_sem.at[target, chunk],
            device_id=to, device_id_type=MESH,
        )

    def arrived(source, chunk):
        gather_copy(source, source, chunk, (ring, me), send_sem.at[0, 0]).wait_recv()

    if paired:
        far = pl.ds(pl.multiple_of(side * 2 * stripe, stripe), 2 * stripe)

        def teach_send(cols, dst, to, k):
            return pltpu.make_async_remote_copy(
                src_ref=teacher_in.at[0, :, cols], dst_ref=dst, send_sem=teach_send_sem.at[k],
                recv_sem=teach_recv_sem.at[k], device_id=to, device_id_type=MESH,
            )

        to_swap = teach_send(far, teach.at[:, far], (buddy, flip2(me)), 0)
        to_near = teach_send(rows_of(flip2(me)), near.at[0], (buddy, me), 1)
        to_next = teach_send(rows_of(flip3(me)), near.at[1], (buddy, flip1(me)), 2)
        far_in = pl.ds(pl.multiple_of((1 - side) * 2 * stripe, stripe), 2 * stripe)

        def to_x(chunk):
            return gather_copy(base_at, base_at, chunk, (ring, flip1(me)), send_sem.at[0, chunk])

        def to_buddy(chunk):
            return gather_copy(base_at, base_at, chunk, (buddy, me), send_sem.at[1, chunk])

        def pass_on(chunk):
            return gather_copy(flip1(base_at), flip1(base_at), chunk, (buddy, me), send_sem.at[2, chunk])

        def swap(chunk):
            return gather_copy(groups, me, chunk, (buddy, flip2(me)), send_sem.at[3, chunk])

        order = (flip1(me), flip3(me), me, flip2(me))
        pl.semaphore_wait(barrier, greeted)

        @pl.when(is_home)
        def _():
            to_near.start()
            to_next.start()

        for chunk in order:
            conv_chunk(chunk)

            @pl.when(is_home)
            def _(chunk=chunk):
                to_x(chunk).start()
                to_buddy(chunk).start()

            @pl.when(is_guest)
            def _(chunk=chunk):
                swap(chunk).start()

        @pl.when(is_guest)
        def _():
            to_swap.start()
            for chunk in (flip3(me), flip1(me), flip2(me), me):
                arrived(base_at, chunk)
                to_x(chunk).start()
                to_buddy(chunk).start()
            for k in range(2):
                teach_send(rows_of(0), near.at[k], (ring, me), 1 + k).wait_recv()
                at = me if k == 0 else flip1(me)

                def turn(i, _, k=k, at=at):
                    rows = pl.ds(pl.multiple_of(i * 128, 128), 128)
                    for c in range(0, stripe, 128):
                        cols = pl.ds(pl.multiple_of(at * stripe + c, 128), 128)
                        teach[rows, cols] = near[k, c : c + 128, rows].T
                    return 0

                lax.fori_loop(0, stripe // 128, turn, 0)

        for chunk in (base_at, flip2(base_at)):
            arrived(flip1(base_at), chunk)
            pass_on(chunk).start()
    else:
        for c in range(groups):
            conv_chunk(c)
        pl.semaphore_wait(barrier, greeted)

        def send_all(copy_do):
            def body(i, _):
                chunk, step = i // (groups - 1), 1 + lax.rem(i, groups - 1)
                copy_do(gather_copy(me, me, chunk, (ring, lax.rem(me + step, groups)), send_sem.at[step, chunk]))
                return 0

            lax.fori_loop(0, groups * (groups - 1), body, 0)

        send_all(lambda copy: copy.start())

    def wait_chunk(t, chunk):
        if paired:
            @pl.when(t >= 2)
            def _():
                arrived(flip1(base_at), chunk)
                pass_on(chunk).start()

            arrived(flip2(base_at), chunk)
            arrived(flip3(base_at), chunk)
        else:
            def body(step, _):
                arrived(lax.rem(me + step, groups), chunk)
                return 0

            lax.fori_loop(1, groups, body, 0)

    norm_tile = min(32, stripe)

    def scale_of(base):
        squares = jnp.zeros((norm_tile, width), f32)
        for g in range(groups):
            block = held[g, pl.ds(base, norm_tile)].astype(f32)
            squares = squares + block * block
        return lax.rsqrt(jnp.sum(squares, axis=1, keepdims=True) / full + epsilon)

    def normalize(chunk, dest):
        def body(i, _):
            base = pl.multiple_of(chunk * stripe + i * norm_tile, norm_tile)
            inverse = scale_of(base)
            for g in range(groups):
                block = held[g, pl.ds(base, norm_tile)].astype(f32)
                dest[pl.ds(pl.multiple_of(i * norm_tile, norm_tile), norm_tile), g * width : (g + 1) * width] = (
                    block * inverse
                ).astype(bf16)
            return 0

        lax.fori_loop(0, stripe // norm_tile, body, 0)

    if paired:
        pl.when(is_home)(teach_copy.wait)

        @pl.when(is_guest)
        def _():
            teach_send(far_in, teach.at[:, far_in], (ring, me), 0).wait_recv()
    else:
        teach_copy.wait()
    mat = min(256, stripe)

    def gram_chunk(t, _):
        if paired:
            late = jnp.where(t == 2, flip3(me), flip1(me))
            chunk = jnp.where(t == 0, base_at, jnp.where(t == 1, flip2(base_at), late))
        else:
            chunk = lax.rem(me + t, groups)
        wait_chunk(t, chunk)
        normalize(chunk, block_n)

        @pl.when(t == 0)
        def _():
            own_n[...] = block_n[...]

        def body(m, _):
            rows = pl.ds(pl.multiple_of(m * mat, mat), mat)
            similarity = lax.dot_general(
                own_n[rows], block_n[...], (((1,), (1,)), ((), ())), preferred_element_type=f32
            ) / full
            residue = (factor * (similarity - teach[rows, rows_of(chunk)])).astype(bf16)
            total[rows] += jnp.dot(residue, block_n[...], preferred_element_type=f32)
            return 0

        lax.fori_loop(0, stripe // mat, body, 0)
        return 0

    lax.fori_loop(0, groups, gram_chunk, 0)

    def finish(i, _):
        local = pl.multiple_of(i * norm_tile, norm_tile)
        base = pl.multiple_of(base_at * stripe + i * norm_tile, norm_tile)
        rows = pl.ds(local, norm_tile)
        inverse = scale_of(base)
        inner = jnp.zeros((norm_tile, width), f32)
        for g in range(groups):
            part = slice(g * width, (g + 1) * width)
            inner = inner + held[g, pl.ds(base, norm_tile)].astype(f32) * inverse * total[rows, part]
        projection = jnp.sum(inner, axis=1, keepdims=True) / full
        for g in range(groups):
            part = slice(g * width, (g + 1) * width)
            normed = held[g, pl.ds(base, norm_tile)].astype(f32) * inverse
            outgoing[g, rows] = (inverse * (total[rows, part] - normed * projection)).astype(bf16)
        return 0

    pieces = max(1, min(4, stripe // 128))
    piece = stripe // pieces
    steps = piece // norm_tile

    def exchange(target, p, source_row):
        return pltpu.make_async_remote_copy(
            src_ref=outgoing.at[target, pl.ds(p * piece, piece)],
            dst_ref=hgrad.at[rows_of(source_row, piece, p * piece)],
            send_sem=a2a_send.at[target, p], recv_sem=a2a_recv.at[source_row, p],
            device_id=(proc, target), device_id_type=MESH,
        )

    if paired:
        targets = (flip3(me), flip1(me), flip2(me))
    else:
        targets = tuple(lax.rem(me + groups - step, groups) for step in range(1, groups))

    def stay(p):
        hgrad[rows_of(base_at, piece, p * piece)] = outgoing[me, pl.ds(p * piece, piece)]

    for p in reversed(range(pieces)):
        lax.fori_loop(p * steps, (p + 1) * steps, finish, 0)
        for target in targets:
            exchange(target, p, base_at).start()
        if paired:
            @pl.when(is_guest)
            def _(p=p):
                exchange(me, p, base_at).start()

            @pl.when(is_home)
            def _(p=p):
                stay(p)
        else:
            stay(p)

    def back_tile(base):
        for k in range(0, width, 128):
            lane = slice(k, min(k + 128, width))
            up = hgrad[pl.ds(base, tile + PAD), lane].astype(f32)
            for b, (conv, raw, weights, store) in enumerate(
                ((conv_v, raw_g, filter_gate, gate_out), (conv_g, raw_v, filter_value, value_out))
            ):
                window = up * conv[pl.ds(base, tile + PAD), lane]
                signal = raw[pl.ds(pl.multiple_of(base + PAD, PAD), tile), lane].astype(f32)
                out = None
                for j in range(taps):
                    shifted = (window if j == 0 else pltpu.roll(window, tile + PAD - j, 0))[:tile]
                    term = weights[j : j + 1, lane] * shifted
                    out = term if out is None else out + term
                    product = shifted * signal
                    folded = product[0:8]
                    for r in range(8, tile, 8):
                        folded = folded + product[r : r + 8]
                    sums[b, j, :, lane] += folded
                store[0, pl.ds(base, tile), lane] = out.astype(bf16)

    tiles = stripe // tile
    per = tiles // pieces
    if paired:
        sources = (base_at, flip2(base_at), flip1(base_at), flip3(base_at))
    else:
        sources = tuple(lax.rem(me + step, groups) for step in range(groups))
    for p in reversed(range(pieces)):
        for step, source in enumerate(sources):
            def landed(p=p, source=source):
                exchange(source, p, source).wait_recv()

            if step:
                landed()
            elif paired:
                pl.when(is_guest)(landed)

            def inner_tiles(i, _, source=source):
                back_tile(pl.multiple_of(source * stripe + i * tile, tile))
                return 0

            lax.fori_loop(p * per, (p + 1) * per - (1 if p == pieces - 1 else 0), inner_tiles, 0)

    def last_tiles(c, _):
        back_tile(pl.multiple_of(c * stripe + (tiles - 1) * tile, tile))
        return 0

    lax.fori_loop(0, groups, last_tiles, 0)
    for b in range(2):
        for j in range(taps):
            mine[b, j : j + 1] = jnp.sum(sums[b, j], axis=0, keepdims=True)
        mine[b, taps:] = jnp.zeros((8 - taps, width), f32)

    def tap_copy(to, slot):
        return pltpu.make_async_remote_copy(
            src_ref=mine, dst_ref=others.at[slot], send_sem=tap_send.at[slot], recv_sem=tap_recv.at[slot],
            device_id=(to, me), device_id_type=MESH,
        )

    tap_copies = [tap_copy(lax.rem(ring + step, rings), step) for step in range(1, rings)]
    for copy in tap_copies:
        copy.start()
    summed = [mine[b] for b in range(2)]
    for step, copy in enumerate(tap_copies):
        copy.wait_recv()
        summed = [summed[b] + others[step + 1, b] for b in range(2)]
    gate_taps[...] = summed[0][:taps] * norm_factor
    value_taps[...] = summed[1][:taps] * norm_factor

    for copy in tap_copies:
        copy.wait_send()
    if paired:
        for chunk in range(groups):
            to_x(chunk).wait_send()
            to_buddy(chunk).wait_send()
            pass_on(chunk).wait_send()

        @pl.when(is_home)
        def _():
            to_near.wait_send()
            to_next.wait_send()

        @pl.when(is_guest)
        def _():
            to_swap.wait_send()
            for chunk in range(groups):
                swap(chunk).wait_send()
            for p in range(pieces):
                exchange(me, p, base_at).wait_send()
    else:
        send_all(lambda copy: copy.wait_send())
    for target in targets:
        for p in range(pieces):
            exchange(target, p, base_at).wait_send()


def on_device(gate_raw, value_raw, filter_gate, filter_value, teacher):
    seq_count, length, width = gate_raw.shape
    groups, rings = lax.axis_size("chan"), lax.axis_size("seq")
    taps = filter_gate.shape[0]
    stripe, full = length // groups, width * groups
    norm_factor = 1.0 / math.sqrt(rings * seq_count * length)
    f32, bf16 = jnp.float32, jnp.bfloat16
    any_space = pl.BlockSpec(memory_space=pl.ANY)
    vmem = pl.BlockSpec(memory_space=pltpu.VMEM)
    dma = pltpu.SemaphoreType.DMA
    return pl.pallas_call(
        functools.partial(kernel, groups, rings, taps, norm_factor),
        out_shape=(
            pltpu.VMEM(gate_raw.shape, bf16),
            pltpu.VMEM(gate_raw.shape, bf16),
            jax.ShapeDtypeStruct((taps, width), f32),
            jax.ShapeDtypeStruct((taps, width), f32),
        ),
        in_specs=[any_space, any_space, vmem, vmem, any_space],
        out_specs=(vmem, vmem, vmem, vmem),
        scratch_shapes=[
            pltpu.VMEM((length + PAD, width), bf16),
            pltpu.VMEM((length + PAD, width), bf16),
            pltpu.VMEM((length + PAD, width), f32),
            pltpu.VMEM((length + PAD, width), f32),
            pltpu.VMEM((groups + 1, length, width), bf16),
            pltpu.VMEM((stripe, length), f32),
            pltpu.VMEM((stripe, full), bf16),
            pltpu.VMEM((stripe, full), bf16),
            pltpu.VMEM((stripe, full), f32),
            pltpu.VMEM((groups, stripe, width), bf16),
            pltpu.VMEM((length + PAD, width), bf16),
            pltpu.VMEM((2, taps, 8, width), f32),
            pltpu.VMEM((2, 8, width), f32),
            pltpu.VMEM((rings, 2, 8, width), f32),
            dma((3, groups)),
            dma((groups, groups)),
            dma((groups, groups)),
            dma((groups, 4)),
            dma((groups, 4)),
            dma((rings,)),
            dma((rings,)),
            pltpu.VMEM((2, stripe, stripe), f32),
            dma((3,)),
            dma((3,)),
        ],
        compiler_params=pltpu.CompilerParams(
            collective_id=0, has_side_effects=True, vmem_limit_bytes=52 * 1024 * 1024
        ),
    )(gate_raw, value_raw, filter_gate, filter_value, teacher)


def solution(mesh):
    placed = (
        P("seq", None, "chan"),
        P("seq", None, "chan"),
        P(None, "chan"),
        P(None, "chan"),
        P("seq", "chan", None),
    )
    return jax.shard_map(
        on_device,
        mesh=mesh,
        in_specs=placed,
        out_specs=(
            P("seq", None, "chan"),
            P("seq", None, "chan"),
            P(None, "chan"),
            P(None, "chan"),
        ),
        check_vma=False,
    )
```
